32 devices in a mesh: row: 4 (over z), col: 8 (over y, x, core).
Axes of the slice: x: 2, y: 2, z: 4, core: 2. Of those that a mesh axis runs over, the one named last changes fastest.
Arguments:
- velocity: bfloat16 [3, 8, 2048, 2048], P(None, 'col', 'row'), may hold values from -6 to 6
- vorticity: bfloat16 [3, 8, 2048, 2048], P(None, 'col', 'row'), may hold values from -6 to 6
- eddy_state: bfloat16 [8, 64, 3072], P('col', 'row'), may hold values from -0.359375 to 0.359375
- eddy_rate: bfloat16 [8, 64], P('col', 'row'), may hold values from 8 to 64
- block_owner: int32 [8, 4, 64, 1], P('col', 'row'), may hold values from 0 to 3; in each aligned block of 64 rows (0 to 63, 64 to 127, ..., all dimensions but the last counted through in order) at most 32 rows name the same one
- block_slot: int32 [8, 4, 64], P('col', 'row'), may hold values from 0 to 15
Outputs:
- spectral: float32 [3, 8, 1638400], P(None, None, ('row', 'col'))
The draws below stay inside these ranges and needn't reach their ends.
Inputs may be any that keep to these rules, and one draw needn't show every extreme that they name: `block_owner`: among the 64 blocks of one DNS device, at most 32 have the same owner.
All inputs are finite; a program needn't handle non-finite values.
Results may differ from the reference program's by a relative error of at most 0.013.
Values may be sent and summed in bfloat16 or wider, within the bound.
A program may use at most 128 MiB of HBM per device.

```python
import math
import jax
import jax.numpy as jnp
import numpy as np
from jax import lax

NX = 2048
NY = 2048
KXM = 640
KYM = 1280
RATIO = 4
BY = 8
BX = 128
S = 16
ZD = 1
ZW = 8
XC = 512
YC = 128
NB = 64
BLKV = 3072
CAP = 32
KXD = 160
KYD = 160
MODES = 1638400
N_ROW = 4
N_COL = 8


def with_ends(values, key, low, largest):
    extent = values.shape
    place = [jax.random.randint(jax.random.fold_in(key, axis), (), 0, extent[axis]) for axis in range(len(extent))]
    values = values.at[tuple(place)].set(low)
    longest = extent.index(max(extent))
    place[longest] = (place[longest] + 1) % extent[longest]
    return values.at[tuple(place)].set(largest)


def block_scale(key, extent, split, smallest, top_value):
    loudness, own = 1.0, jax.random.fold_in(key, 6)
    for dim, blocks in split:
        draws = jnp.exp(jax.random.uniform(jax.random.fold_in(own, dim), (blocks,), jnp.float32, smallest / len(split), top_value / len(split)))
        loudness = loudness * jnp.repeat(draws, extent[dim] // blocks).reshape([-1 if axis == dim else 1 for axis in range(len(extent))])
    return loudness


def deal_out(stream_key, own, number, rows, count, top, reach, lean):
    ranking = jax.random.permutation(stream_key, count)
    packed, common = load_shares(count, rows * top, reach, lean, True), load_shares(count, rows * top, reach, lean, False)
    places = jnp.arange(count)

    def named(tallies, offset_by):
        used = int((tallies > 0).sum())
        fixed = max(1, used // 4)
        passed = fixed + (places - fixed + offset_by * (used - fixed)) % max(1, count - fixed)
        return jnp.zeros((count,), jnp.int32).at[ranking[jnp.where(places < fixed, places, passed)]].set(jnp.asarray(tallies, jnp.int32))

    tallies = jnp.where(number % 4 == 0, named(packed, number // 4), named(common, number - number // 4 - 1))
    mixed = jax.random.permutation(jax.random.fold_in(own, 3), count)
    giver, receiver = mixed[0:count // 2 * 2:2], mixed[1:count // 2 * 2:2]
    slack = jnp.minimum(tallies[giver] - 1, reach - tallies[receiver]) // 2
    slack = jnp.where((giver == ranking[0]) | (receiver == ranking[0]) | (tallies[receiver] == 0), 0, jnp.maximum(slack, 0))
    passed = jax.random.randint(jax.random.fold_in(own, 4), (count // 2,), 0, 1 << 20) % (slack + 1)
    tallies = tallies.at[giver].add(-passed).at[receiver].add(passed)
    items = jnp.searchsorted(jnp.cumsum(tallies), jnp.arange(rows * top), side="right").astype(jnp.int32)
    listing = items.reshape(top, rows).T
    listing = listing[jax.random.permutation(jax.random.fold_in(own, 1), rows)]
    offset_by = jax.random.randint(jax.random.fold_in(own, 2), (rows, 1), 0, top)
    return jnp.take_along_axis(listing, (jnp.arange(top)[None, :] + offset_by) % top, axis=1)


def load_shares(amount, total, most, slope, full):
    portions = [(1 << 20) // math.isqrt(rank ** slope) + 1 for rank in range(1, amount + 1)]
    largest = most if full else min(most, max(-(-total // amount), total * portions[0] // sum(portions)))
    least = 1 if total - largest >= amount - 1 else 0
    holding, spare = [largest] + [least] * (amount - 1), total - largest - least * (amount - 1)
    while spare > 0:
        free = [i for i in range(1, amount) if holding[i] < largest] or [i for i in range(1, amount) if holding[i] < most]
        pool, left = sum([portions[i] for i in free]), spare
        for i in free:
            addition = min(most - holding[i], max(1, left * portions[i] // pool), spare)
            holding[i] = holding[i] + addition
            spare = spare - addition
    return np.array(holding)


def bell_draw(own_key, shape, deviation, most, cuts=(), kind=jnp.bfloat16):
    gain = block_scale(own_key, shape, cuts, -0.22, 0.18) if cuts else 1.0
    values = jax.random.normal(own_key, shape, jnp.float32) * deviation * gain
    return jnp.minimum(jnp.maximum(values, -most), most).astype(kind)


def setup_inputs(seed: int = 0) -> dict:
    key_list = jax.random.split(jax.random.key(seed), 7)
    velocity = bell_draw(key_list[0], (3, ZW, NY, NX), 1.0, 6.0, ((1, 8), (2, 4)))
    vorticity = bell_draw(key_list[1], (3, ZW, NY, NX), 1.0, 6.0, ((1, 8), (2, 4)))
    eddy_state = bell_draw(key_list[2], (N_COL, N_ROW * S, BLKV), 0.06, 0.359375, ((0, 8), (1, 4)))
    eddy_rate = jnp.clip(jnp.exp(math.log(64.0) - 2.0794415 * jax.random.uniform(key_list[3], (N_COL, N_ROW * S), jnp.float32) ** block_scale(key_list[3], (N_COL, N_ROW * S), ((0, 8), (1, 4)), -0.2, 0.2)), 8.0, 64.0).astype(jnp.bfloat16)
    block_owner_keys = jax.random.split(jax.random.fold_in(key_list[4], 1), N_COL * N_ROW * NB // NB)
    block_owner_turns = jax.random.permutation(jax.random.fold_in(key_list[4], 3), N_COL * N_ROW * NB // NB)
    block_owner = jax.vmap(lambda own, number: deal_out(jax.random.fold_in(key_list[4], 2), own, number, NB, N_ROW, 1, CAP, 2))(block_owner_keys, block_owner_turns).reshape((N_COL, N_ROW, NB, 1))
    block_slot = with_ends(jax.random.randint(key_list[5], (N_COL, N_ROW, NB), 0, S), jax.random.fold_in(key_list[5], 1), 0, S - 1).astype(jnp.int32)
    return {"velocity": velocity, "vorticity": vorticity, "eddy_state": eddy_state, "eddy_rate": eddy_rate, "block_owner": block_owner, "block_slot": block_slot}


section_step = 0.5
viscous_step = 0.15
vertical_step = 0.5

def gauss_value(position, ratio):
    spread = 4.0 * ratio * ratio
    taps = jnp.arange(5 * ratio).astype(jnp.float32)
    shifted = taps - 2.0 * ratio - (ratio - 1) / 2.0
    total = jnp.sum(jnp.exp(-shifted * shifted / (2.0 * spread)))
    moved = position - 2.0 * ratio - (ratio - 1) / 2.0
    return jnp.exp(-moved * moved / (2.0 * spread)) / total

def x_weights(points, coarse, ratio):
    fine = jnp.arange(points, dtype=jnp.int32)[:, None]
    cells = jnp.arange(coarse, dtype=jnp.int32)[None, :]
    offset = jnp.mod(fine - ratio * cells + 2 * ratio, points)
    value = gauss_value(offset.astype(jnp.float32), ratio)
    return jnp.where(offset < 5 * ratio, value, 0.0).astype(jnp.bfloat16)

def x_table(points, kept):
    fine = jnp.arange(points, dtype=jnp.int32)[:, None]
    column = jnp.arange(2 * kept, dtype=jnp.int32)[None, :]
    phase = jnp.mod(column // 2 * fine, points).astype(jnp.float32) * (2.0 * math.pi / points)
    value = jnp.where(column % 2 == 0, jnp.cos(phase), -jnp.sin(phase))
    return (value / math.sqrt(points)).astype(jnp.bfloat16)

def y_tables(points, kept, first, count):
    fine = jnp.arange(points, dtype=jnp.int32)[:, None]
    wave = jnp.arange(count, dtype=jnp.int32)[None, :] + (first - kept // 2)
    phase = jnp.mod(wave * fine, points).astype(jnp.float32) * (2.0 * math.pi / points)
    scale = 1.0 / math.sqrt(points)
    return ((jnp.cos(phase) * scale).astype(jnp.bfloat16), (jnp.sin(phase) * scale).astype(jnp.bfloat16))

def vertical_inverse(planes):
    index = jnp.arange(planes)
    ends = (index == 0) | (index == planes - 1)
    diagonal = jnp.where(ends, 1.0 + vertical_step, 1.0 + 2.0 * vertical_step).astype(jnp.float32)
    lower = jnp.where(index == 0, 0.0, -vertical_step).astype(jnp.float32)
    upper = jnp.where(index == planes - 1, 0.0, -vertical_step).astype(jnp.float32)
    return lax.linalg.tridiagonal_solve(lower, diagonal, upper, jnp.eye(planes, dtype=jnp.float32))

def damping(x_wave, y_wave, points_x, points_y):
    angle_x = x_wave.astype(jnp.float32) * (2.0 * math.pi / points_x)
    angle_y = y_wave.astype(jnp.float32) * (2.0 * math.pi / points_y)
    total = angle_y[:, None, None] * angle_y[:, None, None] + angle_x[None, None, :] * angle_x[None, None, :]
    return jnp.broadcast_to(jnp.exp(-viscous_step * total), (y_wave.shape[0], 2, x_wave.shape[0]))

def reference(velocity, vorticity, eddy_state, eddy_rate, block_owner, block_slot):
    highest = lax.Precision.HIGHEST
    xweights = x_weights(NX, XC, RATIO).astype(jnp.float32)
    taps = gauss_value(jnp.arange(5 * RATIO).astype(jnp.float32), RATIO)
    taps = lax.optimization_barrier(taps.astype(jnp.bfloat16)).astype(jnp.float32)
    xtable = x_table(NX, KXM).astype(jnp.float32)
    ycos, ysin = y_tables(NY, KYM, 0, KYM)
    ycos = ycos.astype(jnp.float32)
    ysin = ysin.astype(jnp.float32)

    def filter_plane(index):
        plane = lax.dynamic_index_in_dim(velocity, index, 1, keepdims=False).astype(jnp.float32)
        along = jnp.dot(plane.reshape(3 * NY, NX).astype(jnp.float32), xweights.astype(jnp.float32), precision=highest, preferred_element_type=jnp.float32).reshape(3, NY, XC)
        along = lax.optimization_barrier(along.astype(jnp.bfloat16)).astype(jnp.float32)
        total = jnp.zeros((3, NY // RATIO, XC), jnp.float32)
        for tap in range(5 * RATIO):
            moved = jnp.roll(along, 2 * RATIO - tap, axis=1)
            total = total + taps[tap] * moved[:, ::RATIO, :]
        return total.astype(jnp.bfloat16)
    filtered = lax.map(filter_plane, jnp.arange(ZW, dtype=jnp.int32))
    blocks = filtered.reshape(N_COL, ZD, 3, N_ROW, YC // BY, BY, XC // BX, BX)
    blocks = blocks.transpose(0, 3, 1, 4, 6, 2, 5, 7).reshape(N_COL, N_ROW * NB, BLKV)
    owners = block_owner.reshape(N_COL, N_ROW * NB).astype(jnp.int32)
    slots = block_slot.reshape(N_COL, N_ROW * NB).astype(jnp.int32)
    chosen = (owners * S + slots).astype(jnp.int32)
    state = jnp.take_along_axis(eddy_state, chosen[:, :, None], axis=1).astype(jnp.float32)
    rates = jnp.take_along_axis(eddy_rate, chosen, axis=1).astype(jnp.float32)
    forcing_blocks = (rates[:, :, None] * (state - blocks.astype(jnp.float32))).astype(jnp.bfloat16)
    coarse = forcing_blocks.reshape(N_COL, N_ROW, ZD, YC // BY, XC // BX, 3, BY, BX)
    coarse = coarse.transpose(0, 2, 5, 1, 3, 6, 4, 7).reshape(ZW, 3, NY // RATIO, XC)

    def transform_plane(index):
        speed = lax.dynamic_index_in_dim(velocity, index, 1, keepdims=False).astype(jnp.float32)
        spin = lax.dynamic_index_in_dim(vorticity, index, 1, keepdims=False).astype(jnp.float32)
        local = lax.dynamic_index_in_dim(coarse, index, 0, keepdims=False).astype(jnp.float32)
        forcing = jnp.repeat(jnp.repeat(local, RATIO, axis=1), RATIO, axis=2)
        cross = jnp.stack([speed[1] * spin[2] - speed[2] * spin[1], speed[2] * spin[0] - speed[0] * spin[2], speed[0] * spin[1] - speed[1] * spin[0]], axis=0)
        section = (speed + section_step * (cross + forcing)).astype(jnp.bfloat16)
        xspec = jnp.dot(section.reshape(3 * NY, NX).astype(jnp.float32), xtable.astype(jnp.float32), precision=highest, preferred_element_type=jnp.float32).astype(jnp.bfloat16)
        xspec = xspec.reshape(3, NY, KXM, 2).astype(jnp.float32)
        real_in = xspec[:, :, :, 0]
        imag_in = xspec[:, :, :, 1]
        real_out = jnp.einsum('cnk,nj->cjk', real_in, ycos, precision=highest) + jnp.einsum('cnk,nj->cjk', imag_in, ysin, precision=highest)
        imag_out = jnp.einsum('cnk,nj->cjk', imag_in, ycos, precision=highest) - jnp.einsum('cnk,nj->cjk', real_in, ysin, precision=highest)
        return jnp.stack([real_out, imag_out], axis=2).astype(jnp.bfloat16)
    spectrum = lax.map(transform_plane, jnp.arange(ZW, dtype=jnp.int32))
    inverse = vertical_inverse(ZW).astype(jnp.bfloat16).astype(jnp.float32)
    mixed = jnp.einsum('wz,zcjpk->cwjpk', inverse, spectrum.astype(jnp.float32), precision=highest)
    factor = damping(jnp.arange(KXM), jnp.arange(KYM) - KYM // 2, NX, NY)
    result = mixed * factor[None, None]
    result = result.reshape(3, ZW, N_COL, KYD, 2, N_ROW, KXD).transpose(0, 1, 5, 2, 3, 4, 6)
    return result.reshape(3, ZW, MODES)
```

```python
import math

import jax
import jax.numpy as jnp
import numpy as np
from jax import lax
from jax.experimental import pallas as pl
from jax.experimental.pallas import tpu as pltpu
from jax.sharding import PartitionSpec as P

NX = 2048
NY = 2048
KXM = 640
KYM = 1280
RATIO = 4
BY = 8
BX = 128
S = 16
BLKV = 3072


section_step = 0.5
viscous_step = 0.15
vertical_step = 0.5


def padded_2(cells, sides, width):
    for axis, dim in sides:
        count = lax.axis_size(axis)
        head = lax.slice_in_dim(cells, 0, width, axis=dim)
        tail = lax.slice_in_dim(cells, cells.shape[dim] - width, cells.shape[dim], axis=dim)
        cells = jnp.concatenate(
            [
                lax.ppermute(tail, axis, [(i, (i + 1) % count) for i in range(count)]),
                cells,
                lax.ppermute(head, axis, [((i + 1) % count, i) for i in range(count)]),
            ],
            axis=dim,
        )
    return cells


def gauss_value(position, ratio):
    spread = 4.0 * ratio * ratio
    taps = jnp.arange(5 * ratio).astype(jnp.float32)
    shifted = taps - 2.0 * ratio - (ratio - 1) / 2.0
    total = jnp.sum(jnp.exp(-shifted * shifted / (2.0 * spread)))
    moved = position - 2.0 * ratio - (ratio - 1) / 2.0
    return jnp.exp(-moved * moved / (2.0 * spread)) / total


def x_weights(points, coarse, ratio):
    fine = jnp.arange(points, dtype=jnp.int32)[:, None]
    cells = jnp.arange(coarse, dtype=jnp.int32)[None, :]
    offset = jnp.mod(fine - ratio * cells + 2 * ratio, points)
    value = gauss_value(offset.astype(jnp.float32), ratio)
    return jnp.where(offset < 5 * ratio, value, 0.0).astype(jnp.bfloat16)


def y_weights(coarse, padded, ratio):
    cells = jnp.arange(coarse, dtype=jnp.int32)[:, None]
    fine = jnp.arange(padded, dtype=jnp.int32)[None, :]
    offset = fine - ratio * cells
    value = gauss_value(offset.astype(jnp.float32), ratio)
    return jnp.where((offset >= 0) & (offset < 5 * ratio), value, 0.0).astype(jnp.bfloat16)


def x_table(points, kept):
    fine = jnp.arange(points, dtype=jnp.int32)[:, None]
    column = jnp.arange(2 * kept, dtype=jnp.int32)[None, :]
    phase = jnp.mod(column // 2 * fine, points).astype(jnp.float32) * (2.0 * math.pi / points)
    value = jnp.where(column % 2 == 0, jnp.cos(phase), -jnp.sin(phase))
    return (value / math.sqrt(points)).astype(jnp.bfloat16)


def y_tables(points, kept, first, count):
    fine = jnp.arange(points, dtype=jnp.int32)[:, None]
    wave = jnp.arange(count, dtype=jnp.int32)[None, :] + (first - kept // 2)
    phase = jnp.mod(wave * fine, points).astype(jnp.float32) * (2.0 * math.pi / points)
    scale = 1.0 / math.sqrt(points)
    return (
        (jnp.cos(phase) * scale).astype(jnp.bfloat16),
        (jnp.sin(phase) * scale).astype(jnp.bfloat16),
    )


def vertical_inverse(planes):
    index = jnp.arange(planes)
    ends = (index == 0) | (index == planes - 1)
    diagonal = jnp.where(ends, 1.0 + vertical_step, 1.0 + 2.0 * vertical_step).astype(jnp.float32)
    lower = jnp.where(index == 0, 0.0, -vertical_step).astype(jnp.float32)
    upper = jnp.where(index == planes - 1, 0.0, -vertical_step).astype(jnp.float32)
    return lax.linalg.tridiagonal_solve(lower, diagonal, upper, jnp.eye(planes, dtype=jnp.float32))


def damping(x_wave, y_wave, points_x, points_y):
    angle_x = x_wave.astype(jnp.float32) * (2.0 * math.pi / points_x)
    angle_y = y_wave.astype(jnp.float32) * (2.0 * math.pi / points_y)
    total = (
        angle_y[:, None, None] * angle_y[:, None, None]
        + angle_x[None, None, :] * angle_x[None, None, :]
    )
    return jnp.broadcast_to(jnp.exp(-viscous_step * total), (y_wave.shape[0], 2, x_wave.shape[0]))


def along_y(piece):
    items, width, length = piece.shape
    half = width // 2
    split = piece.reshape(items, half, 2, length)
    real_in = split[:, :, 0, :]
    imag_in = split[:, :, 1, :]
    block = 256
    outputs = []
    for first in range(0, KYM, block):
        cosine, sine = y_tables(length, KYM, first, block)
        real_out = jnp.einsum(
            "kin,nj->kji", real_in, cosine, preferred_element_type=jnp.float32
        ) + jnp.einsum("kin,nj->kji", imag_in, sine, preferred_element_type=jnp.float32)
        imag_out = jnp.einsum(
            "kin,nj->kji", imag_in, cosine, preferred_element_type=jnp.float32
        ) - jnp.einsum("kin,nj->kji", real_in, sine, preferred_element_type=jnp.float32)
        outputs.append(jnp.concatenate([real_out, imag_out], axis=2))
    return jnp.concatenate(outputs, axis=1).astype(jnp.bfloat16)


def generic_device(velocity, vorticity, eddy_state, eddy_rate, block_owner, block_slot):
    components, depth, rows, points = velocity.shape
    coarse_rows = rows // RATIO
    coarse_cols = points // RATIO
    xweights = x_weights(points, coarse_cols, RATIO)
    local = jnp.einsum(
        "czyn,nx->czyx", velocity, xweights, preferred_element_type=jnp.float32
    ).astype(jnp.bfloat16)
    along = padded_2(local, (("row", 2),), 2 * RATIO)
    yweights = y_weights(coarse_rows, rows + 4 * RATIO, RATIO)
    filtered = jnp.einsum(
        "iy,czyx->czix", yweights, along, preferred_element_type=jnp.float32
    ).astype(jnp.bfloat16)
    ybands = coarse_rows // BY
    xbands = coarse_cols // BX
    count = depth * ybands * xbands
    blocks = filtered.reshape(components, depth, ybands, BY, xbands, BX).transpose(1, 2, 4, 0, 3, 5)
    blocks = blocks.reshape(count, BLKV)
    owners = block_owner.reshape(count)
    slots = block_slot.reshape(count)
    owners_total = lax.axis_size("row")
    every_state, every_rate = (
        lax.all_gather(eddy_state, "row", axis=1, tiled=True),
        lax.all_gather(eddy_rate, "row", axis=1, tiled=True),
    )
    chosen = owners * S + slots
    lookup = (chosen[:, None] == jnp.arange(owners_total * S, dtype=jnp.int32)[None, :]).astype(
        jnp.bfloat16
    )
    state = jnp.dot(lookup, every_state[0], preferred_element_type=jnp.float32)
    rates = jnp.dot(lookup, every_rate[0][:, None], preferred_element_type=jnp.float32)[:, 0]
    forcing_blocks = (rates[:, None] * (state - blocks.astype(jnp.float32))).astype(jnp.bfloat16)
    coarse = forcing_blocks.reshape(depth, ybands, xbands, components, BY, BX).transpose(
        3, 0, 1, 4, 2, 5
    )
    coarse = coarse.reshape(components, depth, coarse_rows, coarse_cols).astype(jnp.float32)
    forcing = jnp.repeat(jnp.repeat(coarse, RATIO, axis=2), RATIO, axis=3)
    speed = velocity.astype(jnp.float32)
    spin = vorticity.astype(jnp.float32)
    cross = jnp.stack(
        [
            speed[1] * spin[2] - speed[2] * spin[1],
            speed[2] * spin[0] - speed[0] * spin[2],
            speed[0] * spin[1] - speed[1] * spin[0],
        ],
        axis=0,
    )
    section = (speed + section_step * (cross + forcing)).astype(jnp.bfloat16)
    xtable = x_table(points, KXM)
    spectrum = jnp.einsum(
        "kyn,nm->kmy",
        section.reshape(components * depth, rows, points),
        xtable,
        preferred_element_type=jnp.float32,
    ).astype(jnp.bfloat16)
    ordered = along_y(lax.all_to_all(spectrum, "row", split_axis=1, concat_axis=2, tiled=True))
    ordered = ordered.reshape(components, depth, KYM, -1)
    inverse = vertical_inverse(depth * lax.axis_size("col")).astype(jnp.bfloat16)
    mode_rows = KYM // lax.axis_size("col")
    mode_cols = ordered.shape[3] // 2
    x_wave = lax.axis_index("row") * mode_cols + jnp.arange(mode_cols, dtype=jnp.int32)
    y_wave = lax.axis_index("col") * mode_rows + jnp.arange(mode_rows, dtype=jnp.int32) - KYM // 2
    factor = damping(x_wave, y_wave, NX, NY).reshape(-1)
    piece = lax.all_to_all(ordered, "col", split_axis=2, concat_axis=1, tiled=True)
    items = piece.shape[0]
    flat = piece.reshape(items, piece.shape[1], -1)
    mixed = jnp.einsum("wz,kzl->kwl", inverse, flat, preferred_element_type=jnp.float32)
    return mixed * factor[None, None, :]


MESH = pl.DeviceIdType.MESH
F32 = jnp.float32
BF16 = jnp.bfloat16
LANES = 128
HALF = LANES // 2
MARGIN = 32


def fits(rows, points, n_row, n_col):
    mode_cols, mode_rows = KXM // n_row, KYM // n_col
    return (
        n_row == 4
        and n_col == 8
        and rows % 256 == 0
        and points % 1024 == 0
        and points >= 2048
        and mode_cols // HALF == 2
        and mode_cols % HALF == HALF // 2
        and mode_rows % 32 == 0
        and KYM % n_row == 0
        and (KYM // n_row) % 32 == 0
        and KYM // n_row + MARGIN <= rows
    )


def band_basis(rows, points, kept):
    n = np.arange(rows)
    step = np.arange(1, rows)
    off = np.sin(np.pi * step / points) * np.sin(np.pi * (rows - step) / points)
    main = -np.cos(2.0 * np.pi * (n - (rows - 1) / 2.0) / points)
    main = main * np.cos(np.pi * (kept + 1) / points)
    _, vectors = np.linalg.eigh(np.diag(main) + np.diag(off, 1) + np.diag(off, -1))
    basis = vectors[:, ::-1][:, : kept * rows // points + MARGIN]
    side = np.cos(1.0 + 0.7 * n + 0.003 * n * n) @ basis
    return basis * np.where(side < 0, -1.0, 1.0)[None, :]


def x_table_lanes(points, kept, n_row):
    per = kept // n_row
    wave, imag = [], []
    for first, size, lead in ((0, HALF, True), (2 * HALF, per - 2 * HALF, False)):
        for d in range(n_row):
            for ch in range(2 if lead else 1):
                for p in range(2):
                    wave.append(d * per + first + ch * size + np.arange(size))
                    imag.append(np.full(size, p))
    wave, imag = np.concatenate(wave), np.concatenate(imag)
    phase = (np.arange(points)[:, None] * wave[None, :]) % points * (2.0 * math.pi / points)
    value = np.where(imag[None, :] == 0, np.cos(phase), -np.sin(phase)) / math.sqrt(points)
    fine = value.astype(BF16)
    coarse = fine.astype(np.float32).reshape(points // RATIO, RATIO, 2 * kept).sum(1)
    return np.concatenate([fine, (section_step * coarse).astype(BF16)], axis=0)


def y_tables_b(points, kept, basis):
    n = np.arange(basis.shape[0])
    out = []
    for q in range(4):
        wave = 4 * np.arange(kept // 4) + q - kept // 2
        phase = (wave[:, None] * n[None, :]) % points * (2.0 * math.pi / points)
        both = [np.cos(phase) @ basis, np.sin(phase) @ basis]
        out.append(np.concatenate(both, axis=1) / math.sqrt(points))
    return np.stack(out).astype(BF16)


def all_kernel(
    vel, vort, xw, ut, uc, xt, tab, mix, yw, ytop, ybot, eddy, rate, owner, slot, out,
    velv, vortv, xwv, utv, ucv, xtv, tabv, mixv, ywv, ytopv, ybotv,
    along, edges, every, state, picks, flats, coarse, section, projv,
    xsc, xsb, xrc, xrb, ysc, ysb, yrc, yrb, heldc, heldb, fac,
    load_sem, es_sem, er_sem, ss_sem, sr_sem, xs_sem, xr_sem, ys_sem, yr_sem,
):
    me, mc = lax.axis_index("row"), lax.axis_index("col")
    n_row, n_col = xrc.shape[2], yrc.shape[2]
    _, rows, points = velv.shape
    rank = utv.shape[0]
    fold = rank // 2
    cells, lows = points // RATIO, rows // RATIO
    owned = state.shape[2]
    slots = n_row * owned
    barrier = pltpu.get_barrier_semaphore()
    for d in range(1, n_row):
        pl.semaphore_signal(
            barrier, inc=1, device_id={"row": lax.rem(me + d, n_row)}, device_id_type=MESH
        )
    for d in range(1, n_col):
        pl.semaphore_signal(
            barrier, inc=1, device_id={"col": lax.rem(mc + d, n_col)}, device_id_type=MESH
        )
    pairs = [(xw, xwv)] + [(vel.at[c], velv.at[c]) for c in range(3)]
    pairs += [(yw, ywv), (ytop, ytopv), (ybot, ybotv)]
    pairs += [(vort.at[c], vortv.at[c]) for c in (1, 2, 0)]
    pairs += [(ut, utv), (uc, ucv), (xt, xtv), (mix, mixv), (tab, tabv)]
    loads = [pltpu.make_async_copy(a, b, load_sem.at[i]) for i, (a, b) in enumerate(pairs)]
    for load in loads:
        load.start()

    def filter_x(comp):
        for h in range(cells // 256):
            low, high = 256 * RATIO * h - 128, 256 * RATIO * h + 256 * RATIO + 128
            cuts = [(max(low, 0), min(high, points), max(-low, 0))]
            if low < 0:
                cuts.append((points + low, points, 0))
            if high > points:
                cuts.append((0, high - points, points - low))
            total = 0.0
            for start, stop, at in cuts:
                total += jnp.dot(
                    velv[comp, :, start:stop],
                    xwv[at : at + stop - start, :],
                    preferred_element_type=F32,
                )
            along[comp, :, 256 * h : 256 * (h + 1)] = total.astype(BF16)

    def scopy(comp, d):
        return pltpu.make_async_remote_copy(
            src_ref=state.at[comp],
            dst_ref=every.at[comp, :, me],
            send_sem=ss_sem.at[comp, d - 1],
            recv_sem=sr_sem.at[comp, me],
            device_id={"row": lax.rem(me + d, n_row)},
            device_id_type=MESH,
        )

    def ecopy(comp, side):
        dest = lax.rem(me + (1 if side == 0 else n_row - 1), n_row)
        lines = slice(rows - 16, rows) if side == 0 else slice(0, 16)
        return pltpu.make_async_remote_copy(
            src_ref=along.at[comp, lines, :],
            dst_ref=edges.at[side, comp],
            send_sem=es_sem.at[comp, side],
            recv_sem=er_sem.at[comp, side],
            device_id={"row": dest},
            device_id_type=MESH,
        )

    line = lax.broadcasted_iota(jnp.int32, (owned, owned), 0)
    lane = lax.broadcasted_iota(jnp.int32, (owned, owned), 1)
    pace = jnp.where(line == lane, jnp.broadcast_to(rate[...].astype(F32), (owned, owned)), 0.0)
    pace = jnp.broadcast_to(jnp.sum(pace, axis=1, keepdims=True), (owned, BX)).astype(BF16)
    for comp in range(3):
        state[comp, 0] = pace
        for v in range(BY):
            at = (comp * BY + v) * BX
            state[comp, 1 + v] = eddy[:, at : at + BX]
    loads[0].wait()
    loads[1].wait()
    filter_x(0)
    pl.semaphore_wait(barrier, n_row + n_col - 2)

    def spread_out(comp):
        ecopy(comp, 0).start()
        ecopy(comp, 1).start()
        for d in range(1, n_row):
            scopy(comp, d).start()
        every[comp, :, me] = state[comp]

    spread_out(0)
    for comp in range(1, 3):
        loads[1 + comp].wait()
        filter_x(comp)
        spread_out(comp)

    deep = lax.broadcasted_iota(jnp.int32, (lows, BY * slots), 1)
    inner = (lax.broadcasted_iota(jnp.int32, (lows, BY * slots), 0) & (BY - 1)) * slots
    flat = lax.broadcasted_iota(jnp.int32, (lows, slots), 1)
    count = owner.shape[1]
    chosen = jnp.broadcast_to((owner[...] * S + slot[...]).astype(F32), (lows, count))
    block = lax.broadcasted_iota(jnp.int32, (lows, count), 1)
    band = lax.broadcasted_iota(jnp.int32, (lows, count), 0) // BY * (cells // BX)
    for q in range(cells // BX):
        name = jnp.sum(jnp.where(block == band + q, chosen, 0.0), axis=1, keepdims=True)
        name = name.astype(jnp.int32)
        picks[q] = jnp.where(deep == inner + name, 1.0, 0.0).astype(BF16)
        flats[q] = jnp.where(flat == name, 1.0, 0.0).astype(BF16)
    for load in loads[4:12]:
        load.wait()

    far = me // 2
    order = [3 * (1 - far), 2 - far, 1 + 4 * far - me, me]

    def ccopy(comp, ch, k):
        return pltpu.make_async_remote_copy(
            src_ref=xsc.at[comp, ch, k],
            dst_ref=xrc.at[comp, ch, me],
            send_sem=xs_sem.at[comp, ch, k],
            recv_sem=xr_sem.at[comp, ch, me],
            device_id={"row": order[k]},
            device_id_type=MESH,
        )

    def bcopy(comp, k):
        return pltpu.make_async_remote_copy(
            src_ref=xsb.at[comp, order[k]],
            dst_ref=xrb.at[comp, me],
            send_sem=xs_sem.at[comp, 2, k],
            recv_sem=xr_sem.at[comp, 2, me],
            device_id={"row": order[k]},
            device_id_type=MESH,
        )

    def force(comp):
        for d in range(1, n_row):
            source = lax.rem(me + d, n_row)
            pltpu.make_async_remote_copy(
                src_ref=state.at[comp],
                dst_ref=every.at[comp, :, source],
                send_sem=ss_sem.at[comp, d - 1],
                recv_sem=sr_sem.at[comp, source],
                device_id={"row": source},
                device_id_type=MESH,
            ).wait_recv()
        ecopy(comp, 0).wait_recv()
        ecopy(comp, 1).wait_recv()
        total = jnp.dot(ywv[...], along[comp], preferred_element_type=F32)
        total += jnp.dot(ytopv[...], edges[0, comp], preferred_element_type=F32)
        total += jnp.dot(ybotv[...], edges[1, comp], preferred_element_type=F32)
        smooth = total.astype(BF16).astype(F32)
        for q in range(cells // BX):
            pace = jnp.dot(
                flats[q], every[comp, 0].reshape(slots, BX), preferred_element_type=F32
            )
            held_state = jnp.dot(
                picks[q],
                every[comp, 1:].reshape(BY * slots, BX),
                preferred_element_type=F32,
            )
            lanes = slice(q * BX, (q + 1) * BX)
            coarse[:, lanes] = (pace * (held_state - smooth[:, lanes])).astype(BF16)
        projv[:, points:] = jnp.dot(
            ucv[...], coarse[...], preferred_element_type=F32
        ).astype(BF16)

    mid = lax.broadcasted_iota(jnp.int32, (fold, LANES), 1) < HALF

    def xbody(comp, carry):
        b, c = lax.rem(comp + 1, 3), lax.rem(comp + 2, 3)

        def piece(i, inner):
            lines = pl.ds(pl.multiple_of(i * 16, 16), 16)
            cross = velv[b, lines, :].astype(F32) * vortv[c, lines, :].astype(F32)
            cross = cross - velv[c, lines, :].astype(F32) * vortv[b, lines, :].astype(F32)
            section[lines, :] = (velv[comp, lines, :].astype(F32) + section_step * cross).astype(BF16)
            return inner

        lax.fori_loop(0, rows // 16, piece, 0)
        for at in range(0, points, 512):
            projv[:, at : at + 512] = jnp.dot(
                utv[...], section[:, at : at + 512], preferred_element_type=F32
            ).astype(BF16)
        force(comp)

        @pl.when(comp == 0)
        def _():
            loads[12].wait()

        for k in range(n_row):
            at = pl.ds(pl.multiple_of(order[k] * 2 * LANES, 2 * LANES), 2 * LANES)
            total = jnp.dot(projv[...], xtv[:, at], preferred_element_type=F32).astype(BF16)
            if k < n_row - 1:
                xsc[comp, 0, k] = total[:, :LANES]
                xsc[comp, 1, k] = total[:, LANES:]
                ccopy(comp, 0, k).start()
            else:
                xrc[comp, 0, me] = total[:, :LANES]
                xrc[comp, 1, me] = total[:, LANES:]
            if k == 1:
                ccopy(comp, 1, 0).start()
                ccopy(comp, 1, 1).start()
            if k == 2:
                ccopy(comp, 1, 2).start()
        first = 2 * n_row * LANES
        total = jnp.dot(projv[...], xtv[:, first:], preferred_element_type=F32)
        for d in range(n_row):
            part = total[:, d // 2 * LANES : (d // 2 + 1) * LANES]
            low, high = part[:fold], part[fold:]
            if d % 2 == 0:
                both = jnp.where(mid, low, pltpu.roll(high, HALF, 1))
            else:
                both = jnp.where(mid, pltpu.roll(low, HALF, 1), high)
            xsb[comp, d] = both.astype(BF16)
        for k in (2, 0, 1):
            bcopy(comp, k).start()
        xrb[comp, me] = xsb[comp, me]
        return carry

    lax.fori_loop(0, 3, xbody, 0)
    loads[13].wait()
    loads[14].wait()

    part = ysc.shape[3] // 4
    wide = fac.shape[1]
    width = wide // 2
    row = lax.broadcasted_iota(jnp.int32, fac.shape, 0)
    lane = lax.broadcasted_iota(jnp.int32, fac.shape, 1)
    right = jnp.where(lane >= width, 1, 0)
    lane = lane - width * right
    lane = lane - width // 2 * jnp.where(lane >= width // 2, 1, 0)
    angle_x = (me * (width // 2) + lane).astype(F32) * (2.0 * math.pi / NX)
    angle_y = (mc * (4 * part) + 2 * row + right - KYM // 2).astype(F32) * (2.0 * math.pi / NY)
    fac[...] = jnp.exp(-viscous_step * (angle_y * angle_y + angle_x * angle_x))

    flips = [6, 7, 4, 5, 2, 3, 1]

    def ycopy(sent, got, comp, ch, i):
        dest = mc ^ flips[i]
        return pltpu.make_async_remote_copy(
            src_ref=sent.at[dest],
            dst_ref=got.at[mc],
            send_sem=ys_sem.at[comp, ch, i],
            recv_sem=yr_sem.at[comp, ch, mc],
            device_id={"col": dest},
            device_id_type=MESH,
        )

    def ywait(sent, got, comp, ch):
        for i in range(n_col - 1):
            source = mc ^ flips[i]
            pltpu.make_async_remote_copy(
                src_ref=sent.at[source],
                dst_ref=got.at[source],
                send_sem=ys_sem.at[comp, ch, i],
                recv_sem=yr_sem.at[comp, ch, source],
                device_id={"col": source},
                device_id_type=MESH,
            ).wait_recv()

    def xwait(sent, got, comp, ch):
        for d in range(1, n_row):
            source = lax.rem(me + d, n_row)
            pltpu.make_async_remote_copy(
                src_ref=sent,
                dst_ref=got.at[source],
                send_sem=xs_sem.at[comp, ch, 0],
                recv_sem=xr_sem.at[comp, ch, source],
                device_id={"row": source},
                device_id_type=MESH,
            ).wait_recv()

    def quarters(z, turn):
        s02, s13, d02, d13 = z[0] + z[2], z[1] + z[3], z[0] - z[2], z[1] - z[3]
        t13 = turn(d13)
        return [s02 + s13, d02 + t13, s02 - s13, d02 - t13]

    def lanes_of(count):
        return lax.broadcasted_iota(jnp.int32, (count, LANES), 1)

    def turn_c(x):
        moved = pltpu.roll(x, HALF, 1)
        return jnp.where(lanes_of(x.shape[0]) < HALF, moved, -moved)

    def turn_b(x):
        ahead, back = pltpu.roll(x, LANES - HALF // 2, 1), pltpu.roll(x, HALF // 2, 1)
        return jnp.where((lanes_of(x.shape[0]) & (HALF // 2)) == 0, ahead, -back)

    def ystage_c(comp, ch):
        got = xrc.at[comp, ch]
        xwait(xsc.at[comp, ch, 0], got, comp, ch)
        mixed = quarters([xrc[comp, ch, r].astype(F32) for r in range(4)], turn_c)
        results = []
        for q in range(4):
            both = jnp.concatenate([mixed[q], turn_c(mixed[q])], axis=0).astype(BF16)
            results.append(jnp.dot(tabv[q], both, preferred_element_type=F32))
        for d in range(n_col):
            ysc[comp, ch, d] = jnp.concatenate(
                [results[q][d * part : (d + 1) * part] for q in range(4)], axis=0
            ).astype(BF16)
        for i in range(n_col - 1):
            ycopy(ysc.at[comp, ch], yrc.at[comp, ch], comp, ch, i).start()
        yrc[comp, ch, mc] = ysc[comp, ch, mc]

    def ystage_b(comp):
        xwait(xsb.at[comp, 0], xrb.at[comp], comp, 2)
        mixed = quarters([xrb[comp, r].astype(F32) for r in range(4)], turn_b)
        results = []
        for q in range(4):
            stack = []
            for x in (mixed[q], turn_b(mixed[q])):
                moved = pltpu.roll(x, HALF, 1)
                stack += [x, moved] if q % 2 == 0 else [moved, x]
            both = jnp.concatenate(stack, axis=0).astype(BF16)
            results.append(jnp.dot(tabv[q], both, preferred_element_type=F32))
        near = lanes_of(results[0].shape[0]) < HALF
        joined = [jnp.where(near, results[2 * p], results[2 * p + 1]) for p in range(2)]
        for d in range(n_col):
            ysb[comp, d] = jnp.concatenate(
                [joined[p][d * part : (d + 1) * part] for p in range(2)], axis=0
            ).astype(BF16)
        for i in range(n_col - 1):
            ycopy(ysb.at[comp], yrb.at[comp], comp, 2, i).start()
        yrb[comp, mc] = ysb[comp, mc]

    def zstage(comp):
        ywait(ysc.at[comp, 0], yrc.at[comp, 0], comp, 0)
        ywait(ysc.at[comp, 1], yrc.at[comp, 1], comp, 1)
        for blk in range(4 * part // 16):
            cut = slice(blk * 16, (blk + 1) * 16)
            group = jnp.concatenate(
                [yrc[comp, ch, :, cut, :].reshape(n_col * 16, LANES) for ch in range(2)], axis=1
            )
            mixed = jnp.dot(mixv[...], group, preferred_element_type=F32)
            heldc[cut] = mixed.reshape(16, n_col, 2 * LANES)
        ywait(ysb.at[comp], yrb.at[comp], comp, 2)
        for blk in range(2 * part // 16):
            cut = slice(blk * 16, (blk + 1) * 16)
            group = yrb[comp, :, cut, :].reshape(n_col * 16, LANES)
            mixed = jnp.dot(mixv[...], group, preferred_element_type=F32)
            heldb[cut] = mixed.reshape(16, n_col, LANES)
        lane = lanes_of(n_col)
        quarter = HALF // 2

        def split(pair):
            low, high = pair[:, :LANES], pair[:, LANES:]
            real = jnp.where(lane < HALF, low, pltpu.roll(high, HALF, 1))
            imag = jnp.where(lane < HALF, pltpu.roll(low, HALF, 1), high)
            return real, imag

        def body(s, carry):
            for p in range(2):
                re_l, im_l = split(heldc[2 * p * part + s])
                re_r, im_r = split(heldc[(2 * p + 1) * part + s])
                rest = heldb[p * part + s]
                im_l, re_r = pltpu.roll(im_l, quarter, 1), pltpu.roll(re_r, HALF, 1)
                im_r = pltpu.roll(im_r, HALF + quarter, 1)
                line = [
                    re_l,
                    jnp.where(lane < quarter, rest, im_l),
                    jnp.where(lane < quarter, im_l, jnp.where(lane < HALF, rest, re_r)),
                    jnp.where(lane < HALF, re_r, jnp.where(lane < HALF + quarter, rest, im_r)),
                    jnp.where(lane < HALF + quarter, im_r, rest),
                ]
                lanes = pl.ds(pl.multiple_of((2 * s + p) * wide, LANES), wide)
                scale = fac[pl.ds(2 * s + p, 1), :]
                out[comp, :, lanes] = jnp.concatenate(line, axis=1) * scale
            return carry

        lax.fori_loop(0, part, body, 0, unroll=4)

    def ybody(comp, carry):
        lax.fori_loop(0, 2, lambda ch, inner: (ystage_c(comp, ch), inner)[1], 0)
        ystage_b(comp)
        zstage(comp)
        return carry

    lax.fori_loop(0, 3, ybody, 0)

    def finish(comp, carry):
        for d in range(1, n_row):
            scopy(comp, d).wait_send()
        ecopy(comp, 0).wait_send()
        ecopy(comp, 1).wait_send()
        for k in range(n_row - 1):
            ccopy(comp, 0, k).wait_send()
            ccopy(comp, 1, k).wait_send()
            bcopy(comp, k).wait_send()
        for i in range(n_col - 1):
            ycopy(ysc.at[comp, 0], yrc.at[comp, 0], comp, 0, i).wait_send()
            ycopy(ysc.at[comp, 1], yrc.at[comp, 1], comp, 1, i).wait_send()
            ycopy(ysb.at[comp], yrb.at[comp], comp, 2, i).wait_send()
        return carry

    lax.fori_loop(0, 3, finish, 0)


def all_stages(big, small, n_row, n_col):
    vel, vort, xw, ut, uc, xt, tab, mix, yw, ytop, ybot = big
    _, rows, points = vel.shape
    cells, lows = points // RATIO, rows // RATIO
    owned = small[0].shape[0]
    rank = ut.shape[0]
    lines = KYM // n_col
    wide = 4 * KXM // n_row
    dma = pltpu.SemaphoreType.DMA
    scratch = [pltpu.VMEM(a.shape, BF16) for a in big]
    scratch += [
        pltpu.VMEM((3, rows, cells), BF16),
        pltpu.VMEM((2, 3, 16, cells), BF16),
        pltpu.VMEM((3, 1 + BY, n_row, owned, BX), BF16),
        pltpu.VMEM((3, 1 + BY, owned, BX), BF16),
        pltpu.VMEM((cells // BX, lows, BY * n_row * owned), BF16),
        pltpu.VMEM((cells // BX, lows, n_row * owned), BF16),
        pltpu.VMEM((lows, cells), BF16),
        pltpu.VMEM((rows, points), BF16),
        pltpu.VMEM((rank, points + cells), BF16),
        pltpu.VMEM((3, 2, n_row - 1, rank, LANES), BF16),
        pltpu.VMEM((3, n_row, rank // 2, LANES), BF16),
        pltpu.VMEM((3, 2, n_row, rank, LANES), BF16),
        pltpu.VMEM((3, n_row, rank // 2, LANES), BF16),
        pltpu.VMEM((3, 2, n_col, lines, LANES), BF16),
        pltpu.VMEM((3, n_col, lines // 2, LANES), BF16),
        pltpu.VMEM((3, 2, n_col, lines, LANES), BF16),
        pltpu.VMEM((3, n_col, lines // 2, LANES), BF16),
        pltpu.VMEM((lines, n_col, 2 * LANES), F32),
        pltpu.VMEM((lines // 2, n_col, LANES), F32),
        pltpu.VMEM((lines // 2, wide), F32),
        dma((len(big) + 4,)),
        dma((3, 2)),
        dma((3, 2)),
        dma((3, n_row)),
        dma((3, n_row)),
        dma((3, 3, n_row)),
        dma((3, 3, n_row)),
        dma((3, 3, n_col)),
        dma((3, 3, n_col)),
    ]
    anywhere = pl.BlockSpec(memory_space=pl.ANY)
    vmem = pl.BlockSpec(memory_space=pltpu.VMEM)
    return pl.pallas_call(
        all_kernel,
        out_shape=pltpu.VMEM((3, n_col, lines * wide // 2), F32),
        in_specs=[anywhere] * len(big) + [vmem] * len(small),
        out_specs=vmem,
        scratch_shapes=scratch,
        compiler_params=pltpu.CompilerParams(
            collective_id=0, has_side_effects=True, vmem_limit_bytes=54 * 2**20
        ),
        name="all_stages",
    )(*big, *small)


def filter_tables(rows):
    taps = np.arange(5 * RATIO) - 2.0 * RATIO - (RATIO - 1) / 2.0
    value = np.exp(-taps * taps / (8.0 * RATIO * RATIO))
    value = value / value.sum()

    def weights(offset):
        inside = (offset >= 0) & (offset < 5 * RATIO)
        return np.where(inside, value[np.clip(offset, 0, 5 * RATIO - 1)], 0.0).astype(BF16)

    fine = np.arange(256 * RATIO + 256)[:, None] - 128
    xw = weights(fine - RATIO * np.arange(256)[None, :] + 2 * RATIO)
    cell = RATIO * np.arange(rows // RATIO)[:, None] - 2 * RATIO
    yw = weights(np.arange(rows)[None, :] - cell)
    edge = np.arange(16)[None, :]
    return xw, yw, weights(edge - 16 - cell), weights(edge + rows - cell)


def vertical_inverse_np(planes):
    index = np.arange(planes)
    ends = (index == 0) | (index == planes - 1)
    matrix = np.diag(np.where(ends, 1.0 + vertical_step, 1.0 + 2.0 * vertical_step))
    for i in range(planes - 1):
        matrix[i, i + 1] = matrix[i + 1, i] = -vertical_step
    return np.linalg.inv(matrix).astype(np.float32)


def per_device(velocity, vorticity, eddy_state, eddy_rate, block_owner, block_slot):
    components, depth, rows, points = velocity.shape
    n_row, n_col = lax.axis_size("row"), lax.axis_size("col")
    if depth != 1 or not fits(rows, points, n_row, n_col):
        return generic_device(velocity, vorticity, eddy_state, eddy_rate, block_owner, block_slot)
    basis = band_basis(rows, rows * n_row, KYM)
    ut = np.ascontiguousarray(basis.T).astype(BF16)
    uc = ut.astype(np.float32).reshape(ut.shape[0], rows // RATIO, RATIO).sum(2).astype(BF16)
    xw, yw, ytop, ybot = filter_tables(rows)
    mix = np.einsum("vz,ts->tvzs", vertical_inverse_np(n_col), np.eye(16))
    mix = mix.reshape(16 * n_col, n_col * 16).astype(BF16)
    xt = x_table_lanes(points, KXM, n_row)
    tab = y_tables_b(rows * n_row, KYM, basis)
    big = [velocity.reshape(components, rows, points), vorticity.reshape(components, rows, points)]
    big += [jnp.asarray(t) for t in (xw, ut, uc, xt, tab, mix, yw, ytop, ybot)]
    small = [
        eddy_state[0],
        eddy_rate,
        block_owner.reshape(1, -1),
        block_slot.reshape(1, -1),
    ]
    return all_stages(big, small, n_row, n_col)


def solution(mesh):
    return jax.shard_map(
        per_device,
        mesh=mesh,
        in_specs=(
            P(None, "col", "row", None),
            P(None, "col", "row", None),
            P("col", "row", None),
            P("col", "row"),
            P("col", "row", None, None),
            P("col", "row", None),
        ),
        out_specs=P(None, None, ("row", "col")),
        check_vma=False,
    )
```
